32 devices in a mesh: blk: 8 (over y, x, core), head: 4 (over z).
Axes of the slice: x: 2, y: 2, z: 4, core: 2. Of those that a mesh axis runs over, the one named last changes fastest.
Arguments:
- queries: float32 [16, 2048, 128], P('head', 'blk'), may hold values from -6 to 6
- key_rows: float32 [16, 2048, 128], P('head', 'blk'), may hold values from -1 to 1
- value_rows: float32 [16, 2048, 128], P('head', 'blk'), may hold values from -6 to 6
- memory_keys: bfloat16 [16, 16384, 128], P('head', 'blk'), may hold values from -1 to 1
- memory_values: bfloat16 [16, 16384, 128], P('head', 'blk'), may hold values from -6 to 6
- gate_bias: float32 [16], P('head'), may hold values from -2 to 2
- norm_gain: float32 [16, 128], P('head'), may hold values from 0.1 to 1.9
- block_ids: int32 [16, 16], P('blk'), may hold values from 0 to 127, as said below
- drop_seed: int32 [1], replicated, may hold values from 0 to 999999
- out_grad: float32 [16, 2048, 128], P('head', 'blk'), may hold values from -4 to 4
Outputs:
- query_grad: float32 [16, 2048, 128], P('head', 'blk')
- key_grad: float32 [16, 2048, 128], P('head', 'blk')
- value_grad: float32 [16, 2048, 128], P('head', 'blk')
- memory_key_grad: float32 [16, 16384, 128], P('head', 'blk')
- memory_value_grad: float32 [16, 16384, 128], P('head', 'blk')
The draws below stay inside these ranges and needn't reach their ends.
Inputs may be any that keep to these rules, and one draw needn't show every extreme that they name: `block_ids`: memory block m is held by the device of blk index m // 16. Among the 32 ids of the query blocks of one device, at most 5 (counted with repeats) and at most 5 distinct ones are held by any one device.
All inputs are finite; a program needn't handle non-finite values.
Results may differ from the reference program's by a relative error of at most 0.0004.
Values may be sent and summed in bfloat16 or wider, within the bound.
A program may use at most 128 MiB of HBM per device.

```python
import math
import jax
import jax.numpy as jnp
from jax import lax

H = 16
HD = 128
TB = 128
R = 16
S_DEV = 256
MB_DEV = 16
NQB_DEV = 2
L = 2048
NMB = 128
MEMTOK = 16384
N_BLK = 8


def pair_ceiling():
    limit_uniq = max(1, (NQB_DEV * (R - 1) + N_BLK - 2) // (N_BLK - 1))
    largest = 1
    for paired in range(2, min(R, N_BLK) + 1):
        remaining = NQB_DEV * (R - paired)
        if remaining > 0:
            owners_left = N_BLK - paired
            if owners_left < 1:
                return largest
            if (remaining + owners_left - 1) // owners_left > limit_uniq:
                return largest
        largest = paired
    return largest


def draw_block_ids(key, part):
    pair_limit = pair_ceiling()
    hot_owner = jax.random.randint(jax.random.fold_in(key, 11), (), 0, N_BLK).astype(jnp.int32)
    device_keys = jax.random.split(jax.random.fold_in(key, 12), N_BLK)
    single_device = jax.random.randint(jax.random.fold_in(key, 13), (), 0, N_BLK).astype(jnp.int32)

    def one_device(device_key, device_index):
        perm_key, base_key, local_key, pair_key = jax.random.split(device_key, 4)
        shuffled = jax.random.permutation(perm_key, N_BLK - 1).astype(jnp.int32)
        others = shuffled + (shuffled >= hot_owner).astype(jnp.int32)
        owner_order = jnp.concatenate([hot_owner[None], others]).astype(jnp.int32)
        paired = jax.random.randint(pair_key, (), 1, pair_limit + 1).astype(jnp.int32)
        paired = jnp.where(device_index == single_device, jnp.int32(1), paired)
        bases = jax.random.randint(base_key, (N_BLK,), 0, MB_DEV).astype(jnp.int32)
        pair_locals = jax.random.randint(local_key, (R,), 0, MB_DEV).astype(jnp.int32)
        column = jnp.arange(R, dtype=jnp.int32)[None, :]
        query_block = jnp.arange(NQB_DEV, dtype=jnp.int32)[:, None]
        spread_owners = jnp.maximum(N_BLK - paired, 1)
        serial = jnp.maximum(query_block * (R - paired) + (column - paired), 0)
        spread_index = jnp.minimum(paired + serial % spread_owners, N_BLK - 1)
        spread_owner = owner_order[spread_index]
        visits = serial // spread_owners
        spread_ids = spread_owner * MB_DEV + (bases[spread_owner] + visits) % MB_DEV
        pair_owner = owner_order[jnp.minimum(column, N_BLK - 1)]
        pair_ids = pair_owner * MB_DEV + pair_locals[jnp.minimum(column, R - 1)]
        pair_ids = jnp.broadcast_to(pair_ids, (NQB_DEV, R))
        return jnp.where(column < paired, pair_ids, spread_ids).astype(jnp.int32)
    device_numbers = jnp.arange(N_BLK, dtype=jnp.int32)
    return jax.vmap(one_device)(device_keys, device_numbers).reshape(NQB_DEV * N_BLK, R).astype(jnp.int32)


def block_levels(key, shape, cuts, least, high):
    factor_of = 1.0
    for dim, blocks in cuts:
        steps = jax.random.uniform(jax.random.fold_in(jax.random.fold_in(key, 6), dim), (blocks,), jnp.float32, least / len(cuts), high / len(cuts))
        factor_of = factor_of * jnp.repeat(jnp.exp(steps), shape[dim] // blocks).reshape((-1,) + (1,) * (len(shape) - 1 - dim))
    return factor_of


def noise(own_key, shape, scale, limit, cuts=(), kind=jnp.bfloat16):
    factor_of = block_levels(own_key, shape, cuts, -0.22, 0.18) if cuts else 1.0
    values = jax.random.normal(own_key, shape, jnp.float32) * scale * factor_of
    return jnp.minimum(jnp.maximum(values, -limit), limit).astype(kind)


def setup_inputs(seed: int = 0) -> dict:
    key_of = jax.random.split(jax.random.key(seed), 11)
    queries = jnp.clip(jax.random.uniform(key_of[0], (H, L, HD), jnp.float32, -6.0, 6.0) * block_levels(key_of[0], (H, L, HD), ((0, 4), (1, 8)), -0.4, 0.0), -6.0, 6.0)
    key_rows = jnp.clip(jax.random.uniform(key_of[1], (H, L, HD), jnp.float32, -1.0, 1.0) * block_levels(key_of[1], (H, L, HD), ((0, 4), (1, 8)), -0.4, 0.0), -1.0, 1.0)
    value_rows = noise(key_of[2], (H, L, HD), 1.0, 6.0, ((0, 4), (1, 8)), jnp.float32)
    memory_keys = jnp.clip(jax.random.uniform(key_of[3], (H, MEMTOK, HD), jnp.float32, -1.0, 1.0) * block_levels(key_of[3], (H, MEMTOK, HD), ((0, 4), (1, 8)), -0.4, 0.0), -1.0, 1.0).astype(jnp.bfloat16)
    memory_values = noise(key_of[4], (H, MEMTOK, HD), 1.0, 6.0, ((0, 4), (1, 8)))
    gate_bias = jnp.clip(jax.random.uniform(key_of[5], (H,), jnp.float32, -2.0, 2.0) * block_levels(key_of[5], (H,), ((0, 4),), -0.4, 0.0), -2.0, 2.0)
    norm_gain = jnp.clip(1.0 + 0.18 * jax.random.normal(key_of[6], (H, HD), jnp.float32), 0.1, 1.9)
    block_ids = draw_block_ids(jax.random.fold_in(key_of[10], 71), 0)
    drop_seed = jax.random.randint(key_of[8], (1,), 0, 1000000).astype(jnp.int32)
    out_grad = noise(key_of[9], (H, L, HD), 0.3, 4.0, ((0, 4), (1, 8)), jnp.float32)
    return {"queries": queries, "key_rows": key_rows, "value_rows": value_rows, "memory_keys": memory_keys, "memory_values": memory_values, "gate_bias": gate_bias, "norm_gain": norm_gain, "block_ids": block_ids, "drop_seed": drop_seed, "out_grad": out_grad}


highest = lax.Precision.HIGHEST
drop_level = 103
norm_eps = 1e-06

def mix_bits(counter, seed_value):
    state = counter * jnp.int32(-1640531535) + seed_value
    state = state ^ lax.shift_right_logical(state, jnp.int32(15))
    state = state * jnp.int32(739982445)
    state = state ^ lax.shift_right_logical(state, jnp.int32(12))
    state = state * jnp.int32(695872825)
    state = state ^ lax.shift_right_logical(state, jnp.int32(15))
    return jnp.where(state & 1023 >= drop_level, 1.0 / 0.9, 0.0)

def attend(query_rows, key_block, value_block, allowed, score_scale):
    scores = jnp.einsum('hqd,hkd->hqk', query_rows, key_block, precision=highest) * score_scale
    weights = jnp.where(allowed, jnp.exp(scores), 0.0)
    weights = weights / lax.optimization_barrier(jnp.sum(weights, -1, keepdims=True))
    return jnp.einsum('hqk,hkd->hqd', weights, value_block, precision=highest)

def reference(queries, key_rows, value_rows, memory_keys, memory_values, gate_bias, norm_gain, block_ids, drop_seed, out_grad):
    head_count, length, head_width = queries.shape
    block_count = length // TB
    score_scale = 1.0 / math.sqrt(head_width)
    shape = queries.shape
    counter = (lax.broadcasted_iota(jnp.int32, shape, 0) * length + lax.broadcasted_iota(jnp.int32, shape, 1)) * head_width + lax.broadcasted_iota(jnp.int32, shape, 2)
    keep = mix_bits(counter, drop_seed[0]).astype(queries.dtype)
    gate_mix = jax.nn.sigmoid(gate_bias)[:, None, None]

    def forward(query_all, key_all, value_all, mem_key, mem_value):
        zeros_front = jnp.zeros((head_count, S_DEV, head_width), query_all.dtype)
        key_pad = jnp.concatenate([zeros_front, key_all], 1)
        value_pad = jnp.concatenate([zeros_front, value_all], 1)
        key_store = mem_key.reshape(head_count, NMB, TB, head_width)
        value_store = mem_value.reshape(head_count, NMB, TB, head_width)

        def one_block(index):
            start = index * TB
            query_rows = lax.dynamic_slice_in_dim(query_all, start, TB, 1)
            near_keys = lax.dynamic_slice_in_dim(key_pad, start, S_DEV + TB, 1)
            near_values = lax.dynamic_slice_in_dim(value_pad, start, S_DEV + TB, 1)
            row_pos = start + jnp.arange(TB, dtype=jnp.int32)[:, None]
            key_pos = start - S_DEV + jnp.arange(S_DEV + TB, dtype=jnp.int32)[None, :]
            in_window = (key_pos <= row_pos) & (key_pos > row_pos - S_DEV) & (key_pos >= 0)
            local_part = attend(query_rows, near_keys, near_values, in_window[None], score_scale)
            chosen = block_ids[index]
            far_keys = jnp.take(key_store, chosen, axis=1).reshape(head_count, R * TB, head_width)
            far_values = jnp.take(value_store, chosen, axis=1).reshape(head_count, R * TB, head_width)
            memory_part = attend(query_rows, far_keys, far_values, True, score_scale)
            return (local_part, memory_part)
        local_all, memory_all = lax.map(jax.checkpoint(one_block), jnp.arange(block_count, dtype=jnp.int32))
        local_out = jnp.transpose(local_all, (1, 0, 2, 3)).reshape(shape)
        memory_out = jnp.transpose(memory_all, (1, 0, 2, 3)).reshape(shape)
        mixed = gate_mix * local_out + (1.0 - gate_mix) * memory_out
        mean_square = lax.optimization_barrier(jnp.mean(mixed * mixed, axis=(0, 2), keepdims=True))
        normed = norm_gain[:, None, :] * mixed * lax.rsqrt(mean_square + norm_eps)
        return normed * keep
    result, pullback = jax.vjp(forward, queries, key_rows, value_rows, memory_keys.astype(queries.dtype), memory_values.astype(queries.dtype))
    grads = pullback(out_grad)
    return (grads[0], grads[1], grads[2], grads[3], grads[4])
```

```python
import functools
import math

import jax
import jax.numpy as jnp
from jax import lax
from jax.experimental import pallas as pl
from jax.experimental.pallas import tpu as pltpu
from jax.sharding import PartitionSpec as P

H = 16
TB = 128
R = 16
EXTRA = 8

high = lax.Precision.HIGH
drop_level = 103
norm_eps = 1e-06
bf16 = jnp.bfloat16
f32 = jnp.float32


def from_behind(x, axis, by):
    devices = lax.axis_size(axis)
    pairs = [(i, i + by) for i in range(devices) if 0 <= i + by < devices]
    return lax.ppermute(x, axis, pairs)


def mix_bits(counter, seed_value):
    state = counter * jnp.int32(-1640531535) + seed_value
    state = state ^ lax.shift_right_logical(state, jnp.int32(15))
    state = state * jnp.int32(739982445)
    state = state ^ lax.shift_right_logical(state, jnp.int32(12))
    state = state * jnp.int32(695872825)
    state = state ^ lax.shift_right_logical(state, jnp.int32(15))
    return jnp.where(state & 1023 >= drop_level, 1.0 / 0.9, 0.0)


def split(x):
    top = x.astype(bf16)
    return top, (x - top.astype(f32)).astype(bf16)


def dot(a, b, ca, cb):
    return lax.dot_general(a, b, (((ca,), (cb,)), ((), ())), preferred_element_type=f32)


def collect_pairs(ids_ref, list_ref, mb_dev):
    me = lax.axis_index("blk")
    low = me * mb_dev

    def scan(i, count):
        list_ref[count] = i
        ident = ids_ref[i]
        mine = (ident >= low) & (ident < low + mb_dev)
        return count + mine.astype(jnp.int32)

    return lax.fori_loop(0, ids_ref.shape[0], scan, jnp.int32(0)), low


def place(ids_ref, list_ref, low, block_count, i):
    at = list_ref[i]
    block = at // R
    return block // block_count, (block % block_count) * TB, (ids_ref[at] - low) * TB, block % block_count


def far_forward(heads, mb_dev, block_count, scale, ids_ref, q_ref, k_ref, v_ref, out_ref, list_ref):
    out_ref[...] = jnp.zeros_like(out_ref)
    count, low = collect_pairs(ids_ref, list_ref, mb_dev)
    rows = q_ref.shape[2]
    ones = jnp.ones((8, 2 * TB), bf16)

    def step(i, carry):
        dev, q_at, k_at, sub = place(ids_ref, list_ref, low, block_count, i)
        q_rows = pl.ds(pl.multiple_of(q_at, TB), TB)
        k_rows = pl.ds(pl.multiple_of(k_at, TB), TB)
        for h in range(heads):
            q2 = jnp.concatenate(split(q_ref[dev, h, q_rows, :] * scale), 1)
            k = k_ref[h, k_rows, :]
            v = v_ref[h, k_rows, :]
            e = jnp.exp(dot(q2, jnp.concatenate([k, k], 1), 1, 1))
            e2 = jnp.concatenate(split(e), 1)
            out_ref[dev, h, q_rows, :] += dot(e2, jnp.concatenate([v, v], 0), 1, 0)
            out_ref[dev, h, pl.ds(rows + sub, 1), :] += dot(ones, e2, 1, 1)[:1]
        return carry

    lax.fori_loop(0, count, step, 0)


def far_backward(
    heads, mb_dev, block_count, scale, ids_ref, q_ref, g_ref, k_ref, v_ref, dq_ref, dk_ref, dv_ref, list_ref
):
    dq_ref[...] = jnp.zeros_like(dq_ref)
    dk_ref[...] = jnp.zeros_like(dk_ref)
    dv_ref[...] = jnp.zeros_like(dv_ref)
    count, low = collect_pairs(ids_ref, list_ref, mb_dev)
    rows = q_ref.shape[2]

    def step(i, carry):
        dev, q_at, k_at, sub = place(ids_ref, list_ref, low, block_count, i)
        q_rows = pl.ds(pl.multiple_of(q_at, TB), TB)
        k_rows = pl.ds(pl.multiple_of(k_at, TB), TB)
        for h in range(heads):
            qh, ql = split(q_ref[dev, h, q_rows, :] * scale)
            gh, gl = split(g_ref[dev, h, q_rows, :])
            delta = g_ref[dev, h, pl.ds(rows + sub, 1), :]
            rden = g_ref[dev, h, pl.ds(rows + block_count + sub, 1), :]
            k = k_ref[h, k_rows, :]
            v = v_ref[h, k_rows, :]
            st = dot(jnp.concatenate([k, k], 1), jnp.concatenate([qh, ql], 1), 1, 1)
            dp = dot(jnp.concatenate([v, v], 1), jnp.concatenate([gh, gl], 1), 1, 1)
            p = jnp.exp(st) * rden
            ds = p * (dp - delta)
            ph, plo = split(p)
            dh, dl = split(ds)
            dk_ref[h, k_rows, :] += dot(
                jnp.concatenate([dh, dl, dh], 1), jnp.concatenate([qh, qh, ql], 0), 1, 0
            )
            dv_ref[h, k_rows, :] += dot(
                jnp.concatenate([ph, plo, ph], 1), jnp.concatenate([gh, gh, gl], 0), 1, 0
            )
            dq_ref[dev, h, q_rows, :] += dot(
                jnp.concatenate([dh, dl], 0), jnp.concatenate([k, k], 0), 0, 0
            )
        return carry

    lax.fori_loop(0, count, step, 0)


def local(
    queries,
    key_rows,
    value_rows,
    memory_keys,
    memory_values,
    gate_bias,
    norm_gain,
    block_ids,
    drop_seed,
    out_grad,
):
    heads_dev, shard_rows, head_width = queries.shape
    block_count = shard_rows // TB
    score_scale = 1.0 / math.sqrt(head_width)
    blk_count = lax.axis_size("blk")
    blk_index = lax.axis_index("blk")
    mem_rows = memory_keys.shape[1]
    mb_dev = mem_rows // TB
    gate_mix = jax.nn.sigmoid(gate_bias)[:, None, None]
    hb = 2 if heads_dev % 2 == 0 else 1
    ids_all = lax.all_gather(block_ids.reshape(-1), "blk", axis=0, tiled=True)
    all_queries = lax.all_gather(queries, "blk", axis=0)
    prev_keys, prev_values = from_behind((key_rows, value_rows), "blk", 1)

    smem = pl.BlockSpec(memory_space=pltpu.SMEM)
    grid = (heads_dev // hb,)
    q_spec = pl.BlockSpec((blk_count, hb, shard_rows, head_width), lambda i: (0, i, 0, 0))
    x_spec = pl.BlockSpec((blk_count, hb, shard_rows + EXTRA, head_width), lambda i: (0, i, 0, 0))
    m_spec = pl.BlockSpec((hb, mem_rows, head_width), lambda i: (i, 0, 0))
    params = pltpu.CompilerParams(vmem_limit_bytes=56 * 1024 * 1024)
    scratch = [pltpu.SMEM((ids_all.shape[0] + 1,), jnp.int32)]
    tile_flops = 2 * TB * TB * head_width * heads_dev * block_count * R
    partial = pl.pallas_call(
        functools.partial(far_forward, hb, mb_dev, block_count, score_scale),
        grid=grid,
        in_specs=[smem, q_spec, m_spec, m_spec],
        out_specs=x_spec,
        out_shape=jax.ShapeDtypeStruct(
            (blk_count, heads_dev, shard_rows + EXTRA, head_width), f32
        ),
        scratch_shapes=scratch,
        compiler_params=params,
        cost_estimate=pl.CostEstimate(
            flops=8 * tile_flops, bytes_accessed=12 * 2**20, transcendentals=0
        ),
        name="far_forward",
    )(ids_all, all_queries, memory_keys, memory_values)

    near_keys = jnp.concatenate([prev_keys, key_rows], 1)
    near_values = jnp.concatenate([prev_values, value_rows], 1)
    row_pos = jnp.arange(shard_rows, dtype=jnp.int32)[:, None]
    col_pos = jnp.arange(2 * shard_rows, dtype=jnp.int32)[None, :]
    in_window = (
        (col_pos > row_pos)
        & (col_pos <= row_pos + shard_rows)
        & (blk_index * shard_rows - shard_rows + col_pos >= 0)
    )
    near_scores = jnp.einsum("hqd,hkd->hqk", queries, near_keys, precision=high) * score_scale
    near_exp = jnp.where(in_window[None], jnp.exp(near_scores), 0.0)
    near_total = jnp.sum(near_exp, -1, keepdims=True)
    near_weights = near_exp / near_total
    local_out = jnp.einsum("hqk,hkd->hqd", near_weights, near_values, precision=high)

    whole = lax.psum_scatter(partial, "blk", scatter_dimension=0, tiled=False)
    far_total = whole[:, shard_rows : shard_rows + block_count].reshape(heads_dev, shard_rows, 1)
    memory_out = whole[:, :shard_rows] / far_total

    mixed = gate_mix * local_out + (1.0 - gate_mix) * memory_out
    shape = queries.shape
    head_base = lax.axis_index("head") * heads_dev
    token_base = blk_index * shard_rows
    counter = (
        (head_base + lax.broadcasted_iota(jnp.int32, shape, 0)) * (shard_rows * blk_count)
        + token_base
        + lax.broadcasted_iota(jnp.int32, shape, 1)
    ) * head_width + lax.broadcasted_iota(jnp.int32, shape, 2)
    keep = mix_bits(counter, drop_seed[0]).astype(f32)
    scaled_grad = norm_gain[:, None, :] * keep * out_grad
    sums = lax.psum(
        jnp.stack([jnp.sum(mixed * mixed, axis=(0, 2)), jnp.sum(scaled_grad * mixed, axis=(0, 2))]),
        "head",
    )
    feature_count = H * head_width
    inverse = lax.rsqrt(sums[0] / feature_count + norm_eps)[None, :, None]
    mixed_grad = (
        inverse * scaled_grad
        - mixed * inverse * inverse * inverse * (sums[1] / feature_count)[None, :, None]
    )
    near_grad = gate_mix * mixed_grad
    far_grad = (1.0 - gate_mix) * mixed_grad
    far_delta = jnp.sum(far_grad * memory_out, -1)
    tail = jnp.concatenate(
        [
            far_delta.reshape(heads_dev, block_count, TB),
            (1.0 / far_total).reshape(heads_dev, block_count, TB),
            jnp.zeros((heads_dev, EXTRA - 2 * block_count, TB), f32),
        ],
        1,
    )
    all_grad = lax.all_gather(jnp.concatenate([far_grad, tail], 1), "blk", axis=0)
    dq_all, memory_key_grad, memory_value_grad = pl.pallas_call(
        functools.partial(far_backward, hb, mb_dev, block_count, score_scale),
        grid=grid,
        in_specs=[smem, q_spec, x_spec, m_spec, m_spec],
        out_specs=[q_spec, m_spec, m_spec],
        out_shape=[
            jax.ShapeDtypeStruct((blk_count, heads_dev, shard_rows, head_width), f32),
            jax.ShapeDtypeStruct((heads_dev, mem_rows, head_width), f32),
            jax.ShapeDtypeStruct((heads_dev, mem_rows, head_width), f32),
        ],
        scratch_shapes=scratch,
        compiler_params=params,
        cost_estimate=pl.CostEstimate(
            flops=24 * tile_flops, bytes_accessed=24 * 2**20, transcendentals=0
        ),
        name="far_backward",
    )(ids_all, all_queries, all_grad, memory_keys, memory_values)
    far_query_grad = lax.psum_scatter(dq_all, "blk", scatter_dimension=0, tiled=False) * score_scale

    near_delta = jnp.sum(near_grad * local_out, -1, keepdims=True)
    near_dp = jnp.einsum("hqd,hkd->hqk", near_grad, near_values, precision=high)
    near_ds = near_weights * (near_dp - near_delta) * score_scale
    key_part = jnp.einsum("hqk,hqd->hkd", near_ds, queries, precision=high)
    value_part = jnp.einsum("hqk,hqd->hkd", near_weights, near_grad, precision=high)
    back_keys, back_values = from_behind(
        (key_part[:, :shard_rows], value_part[:, :shard_rows]), "blk", -1
    )
    key_grad = key_part[:, shard_rows:] + back_keys
    value_grad = value_part[:, shard_rows:] + back_values
    near_query_grad = jnp.einsum("hqk,hkd->hqd", near_ds, near_keys, precision=high)
    query_grad = near_query_grad + far_query_grad
    return (query_grad, key_grad, value_grad, memory_key_grad, memory_value_grad)


def solution(mesh):
    return jax.shard_map(
        local,
        mesh=mesh,
        in_specs=(
            P("head", "blk", None),
            P("head", "blk", None),
            P("head", "blk", None),
            P("head", "blk", None),
            P("head", "blk", None),
            P("head"),
            P("head", None),
            P("blk", None),
            P(),
            P("head", "blk", None),
        ),
        out_specs=(
            P("head", "blk", None),
            P("head", "blk", None),
            P("head", "blk", None),
            P("head", "blk", None),
            P("head", "blk", None),
        ),
        check_vma=False,
    )
```

```python
import functools
import math

import jax
import jax.numpy as jnp
from jax import lax
from jax.experimental import pallas as pl
from jax.experimental.pallas import tpu as pltpu
from jax.sharding import PartitionSpec as P

H = 16
TB = 128
R = 16
EXTRA = 8

high = lax.Precision.HIGH
drop_level = 103
norm_eps = 1e-06
bf16 = jnp.bfloat16
f32 = jnp.float32


def from_behind(x, axis, by):
    devices = lax.axis_size(axis)
    pairs = [(i, i + by) for i in range(devices) if 0 <= i + by < devices]
    return lax.ppermute(x, axis, pairs)


def mix_bits(counter, seed_value):
    state = counter * jnp.int32(-1640531535) + seed_value
    state = state ^ lax.shift_right_logical(state, jnp.int32(15))
    state = state * jnp.int32(739982445)
    state = state ^ lax.shift_right_logical(state, jnp.int32(12))
    state = state * jnp.int32(695872825)
    state = state ^ lax.shift_right_logical(state, jnp.int32(15))
    return jnp.where(state & 1023 >= drop_level, 1.0 / 0.9, 0.0)


def split(x):
    top = x.astype(bf16)
    return top, (x - top.astype(f32)).astype(bf16)


def dot(a, b, ca, cb):
    return lax.dot_general(a, b, (((ca,), (cb,)), ((), ())), preferred_element_type=f32)


def flip(index, bit):
    return index + bit - 2 * bit * ((index // bit) % 2)


def greet(others):
    barrier = pltpu.get_barrier_semaphore()
    for other in others:
        pl.semaphore_signal(
            barrier, inc=1, device_id={"blk": other}, device_id_type=pl.DeviceIdType.MESH
        )
    pl.semaphore_wait(barrier, len(others))


def sender(send_sems, recv_sems):
    def send(src, dst, index, other):
        copy = pltpu.make_async_remote_copy(
            src_ref=src,
            dst_ref=dst,
            send_sem=send_sems.at[index],
            recv_sem=recv_sems.at[index],
            device_id={"blk": other},
            device_id_type=pl.DeviceIdType.MESH,
        )
        copy.start()
        return copy

    return send


def gather_steps(x_ref, out_ref, send_sems, recv_sems, own_sem):
    me = lax.axis_index("blk")
    side, over_x, over_y = flip(me, 1), flip(me, 2), flip(me, 4)
    far = flip(over_x, 4)
    half = x_ref.shape[0] // 2
    low, high_part = pl.ds(0, half), pl.ds(half, half)
    send = sender(send_sems, recv_sems)
    to_x = send(x_ref, out_ref.at[me], 1, over_x)
    to_y = send(x_ref, out_ref.at[me], 2, over_y)
    to_side = send(x_ref, out_ref.at[me], 0, side)
    own = pltpu.make_async_copy(x_ref, out_ref.at[me], own_sem)
    own.start()
    to_x.wait_recv()
    x_to_y = send(out_ref.at[over_x, high_part], out_ref.at[over_x, high_part], 4, over_y)
    x_to_side = send(out_ref.at[over_x], out_ref.at[over_x], 3, side)
    to_y.wait_recv()
    y_to_x = send(out_ref.at[over_y, low], out_ref.at[over_y, low], 6, over_x)
    y_to_side = send(out_ref.at[over_y], out_ref.at[over_y], 5, side)
    y_to_x.wait_recv()
    low_to_side = send(out_ref.at[far, low], out_ref.at[far, low], 7, side)
    x_to_y.wait_recv()
    high_to_side = send(out_ref.at[far, high_part], out_ref.at[far, high_part], 8, side)
    for copy in (to_side, x_to_side, y_to_side, low_to_side, high_to_side):
        copy.wait()
    for copy in (to_x, to_y, x_to_y, y_to_x):
        copy.wait_send()
    own.wait()


def gather_ids_kernel(x_ref, ids_ref, out_ref, ids_out_ref, send_sems, recv_sems, id_send, id_recv, own_sems):
    me = lax.axis_index("blk")
    count = out_ref.shape[0]
    others = [(me + j) % count for j in range(1, count)]
    greet(others)
    own = pltpu.make_async_copy(ids_ref, ids_out_ref.at[me], own_sems.at[1])
    own.start()
    send = sender(id_send, id_recv)
    copies = [send(ids_ref, ids_out_ref.at[me], j, other) for j, other in enumerate(others)]
    gather_steps(x_ref, out_ref, send_sems, recv_sems, own_sems.at[0])
    for copy in copies:
        copy.wait()
    own.wait()


def gather_kernel(x_ref, out_ref, send_sems, recv_sems, own_sem):
    me = lax.axis_index("blk")
    greet([flip(me, 1), flip(me, 2), flip(me, 4)])
    gather_steps(x_ref, out_ref, send_sems, recv_sems, own_sem)


def gather_blocks(x, collective_id, ids=None):
    count = lax.axis_size("blk")
    if count != 8 or x.shape[0] % 2:
        gathered = lax.all_gather(x, "blk", axis=0)
        return gathered if ids is None else (gathered, lax.all_gather(ids, "blk", axis=0))
    whole = jax.ShapeDtypeStruct((count,) + x.shape, x.dtype)
    any_space = pl.BlockSpec(memory_space=pl.ANY)
    params = pltpu.CompilerParams(collective_id=collective_id, has_side_effects=True)
    sems = [pltpu.SemaphoreType.DMA((9,)), pltpu.SemaphoreType.DMA((9,))]
    cost = pl.CostEstimate(flops=0, bytes_accessed=2**26, transcendentals=0)
    if ids is None:
        return pl.pallas_call(
            gather_kernel,
            in_specs=[any_space],
            out_specs=any_space,
            out_shape=whole,
            scratch_shapes=sems + [pltpu.SemaphoreType.DMA],
            compiler_params=params,
            cost_estimate=cost,
            name="gather_grad",
        )(x)
    return pl.pallas_call(
        gather_ids_kernel,
        in_specs=[any_space, pl.BlockSpec(memory_space=pltpu.VMEM)],
        out_specs=[any_space, pl.BlockSpec(memory_space=pltpu.VMEM)],
        out_shape=[whole, jax.ShapeDtypeStruct((count,) + ids.shape, ids.dtype)],
        scratch_shapes=sems
        + [
            pltpu.SemaphoreType.DMA((count - 1,)),
            pltpu.SemaphoreType.DMA((count - 1,)),
            pltpu.SemaphoreType.DMA((2,)),
        ],
        compiler_params=params,
        cost_estimate=cost,
        name="gather_queries",
    )(x, ids)


def scatter_kernel(
    part_ref, out_ref, side_ref, far_ref, x_ref, y_ref, hop_ref, in_x_ref, in_y_ref, send_sems, recv_sems
):
    me = lax.axis_index("blk")
    side, over_x, over_y = flip(me, 1), flip(me, 2), flip(me, 4)
    far = flip(over_x, 4)
    half = out_ref.shape[0] // 2
    low, high_part = pl.ds(0, half), pl.ds(half, half)
    greet([side, over_x, over_y])
    send = sender(send_sems, recv_sems)
    far_in = send(part_ref.at[flip(far, 1)], side_ref.at[0], 0, side)
    x_in = send(part_ref.at[flip(over_x, 1)], side_ref.at[1], 1, side)
    y_in = send(part_ref.at[flip(over_y, 1)], side_ref.at[2], 2, side)
    own_in = send(part_ref.at[side], side_ref.at[3], 3, side)
    far_in.wait_recv()
    far_ref[...] = part_ref[far] + side_ref[0]
    far_to_x = send(far_ref.at[low], hop_ref.at[0], 4, over_x)
    far_to_y = send(far_ref.at[high_part], hop_ref.at[1], 5, over_y)
    x_in.wait_recv()
    x_ref[...] = part_ref[over_x] + side_ref[1]
    x_low = send(x_ref.at[low], in_x_ref.at[low], 6, over_x)
    y_in.wait_recv()
    y_ref[...] = part_ref[over_y] + side_ref[2]
    y_high = send(y_ref.at[high_part], in_y_ref.at[high_part], 7, over_y)
    far_to_y.wait_recv()
    x_ref[high_part] += hop_ref[1]
    x_high = send(x_ref.at[high_part], in_x_ref.at[high_part], 8, over_x)
    far_to_x.wait_recv()
    y_ref[low] += hop_ref[0]
    y_low = send(y_ref.at[low], in_y_ref.at[low], 9, over_y)
    own_in.wait_recv()
    out_ref[...] = part_ref[me] + side_ref[3]
    x_low.wait_recv()
    out_ref[low] += in_x_ref[low]
    y_high.wait_recv()
    out_ref[high_part] += in_y_ref[high_part]
    x_high.wait_recv()
    out_ref[high_part] += in_x_ref[high_part]
    y_low.wait_recv()
    out_ref[low] += in_y_ref[low]
    for copy in (far_in, x_in, y_in, own_in, far_to_x, far_to_y, x_low, y_high, x_high, y_low):
        copy.wait_send()


def scatter_blocks(parts, collective_id, name):
    count = lax.axis_size("blk")
    if count != 8 or parts.shape[1] % 2:
        return lax.psum_scatter(parts, "blk", scatter_dimension=0, tiled=False)
    shape = parts.shape[1:]
    block = pltpu.VMEM(shape, parts.dtype)
    return pl.pallas_call(
        scatter_kernel,
        in_specs=[pl.BlockSpec(memory_space=pltpu.VMEM)],
        out_specs=pl.BlockSpec(memory_space=pltpu.VMEM),
        out_shape=jax.ShapeDtypeStruct(shape, parts.dtype),
        scratch_shapes=[
            pltpu.VMEM((4,) + shape, parts.dtype),
            block,
            block,
            block,
            pltpu.VMEM((2, shape[0] // 2) + shape[1:], parts.dtype),
            block,
            block,
            pltpu.SemaphoreType.DMA((10,)),
            pltpu.SemaphoreType.DMA((10,)),
        ],
        compiler_params=pltpu.CompilerParams(
            collective_id=collective_id, has_side_effects=True, vmem_limit_bytes=40 * 1024 * 1024
        ),
        cost_estimate=pl.CostEstimate(flops=0, bytes_accessed=2**26, transcendentals=0),
        name=name,
    )(parts)


def collect_pairs(ids_ref, list_ref, mb_dev, block_count):
    me = lax.axis_index("blk")
    low = me * mb_dev
    per_dev = block_count * R

    def scan(i, count):
        list_ref[count] = i
        ident = ids_ref[i // per_dev, 0, i % per_dev]
        mine = (ident >= low) & (ident < low + mb_dev)
        return count + mine.astype(jnp.int32)

    return lax.fori_loop(0, ids_ref.shape[0] * per_dev, scan, jnp.int32(0)), low


def place(ids_ref, list_ref, low, block_count, i):
    at = list_ref[i]
    dev = at // (block_count * R)
    slot = at % (block_count * R)
    sub = slot // R
    return dev, sub * TB, (ids_ref[dev, 0, slot] - low) * TB, sub


def far_forward(heads, mb_dev, block_count, scale, ids_ref, q_ref, k_ref, v_ref, out_ref, list_ref):
    out_ref[...] = jnp.zeros_like(out_ref)
    count, low = collect_pairs(ids_ref, list_ref, mb_dev, block_count)
    rows = q_ref.shape[2]
    ones = jnp.ones((8, 2 * TB), bf16)

    def step(i, carry):
        dev, q_at, k_at, sub = place(ids_ref, list_ref, low, block_count, i)
        q_rows = pl.ds(pl.multiple_of(q_at, TB), TB)
        k_rows = pl.ds(pl.multiple_of(k_at, TB), TB)
        for h in range(heads):
            q2 = jnp.concatenate(split(q_ref[dev, h, q_rows, :] * scale), 1)
            k = k_ref[h, k_rows, :]
            v = v_ref[h, k_rows, :]
            e = jnp.exp(dot(q2, jnp.concatenate([k, k], 1), 1, 1))
            e2 = jnp.concatenate(split(e), 1)
            out_ref[dev, h, q_rows, :] += dot(e2, jnp.concatenate([v, v], 0), 1, 0)
            out_ref[dev, h, pl.ds(rows + sub, 1), :] += dot(ones, e2, 1, 1)[:1]
        return carry

    lax.fori_loop(0, count, step, 0)


def far_backward(
    heads, mb_dev, block_count, scale, ids_ref, q_ref, g_ref, k_ref, v_ref, dq_ref, dk_ref, dv_ref, list_ref
):
    dq_ref[...] = jnp.zeros_like(dq_ref)
    dk_ref[...] = jnp.zeros_like(dk_ref)
    dv_ref[...] = jnp.zeros_like(dv_ref)
    count, low = collect_pairs(ids_ref, list_ref, mb_dev, block_count)
    rows = q_ref.shape[2]

    def step(i, carry):
        dev, q_at, k_at, sub = place(ids_ref, list_ref, low, block_count, i)
        q_rows = pl.ds(pl.multiple_of(q_at, TB), TB)
        k_rows = pl.ds(pl.multiple_of(k_at, TB), TB)
        for h in range(heads):
            qh, ql = split(q_ref[dev, h, q_rows, :] * scale)
            gh, gl = split(g_ref[dev, h, q_rows, :])
            delta = g_ref[dev, h, pl.ds(rows + sub, 1), :]
            rden = g_ref[dev, h, pl.ds(rows + block_count + sub, 1), :]
            k = k_ref[h, k_rows, :]
            v = v_ref[h, k_rows, :]
            st = dot(jnp.concatenate([k, k], 1), jnp.concatenate([qh, ql], 1), 1, 1)
            dp = dot(jnp.concatenate([v, v], 1), jnp.concatenate([gh, gl], 1), 1, 1)
            p = jnp.exp(st) * rden
            ds = p * (dp - delta)
            ph, plo = split(p)
            dh, dl = split(ds)
            dk_ref[h, k_rows, :] += dot(
                jnp.concatenate([dh, dl, dh], 1), jnp.concatenate([qh, qh, ql], 0), 1, 0
            )
            dv_ref[h, k_rows, :] += dot(
                jnp.concatenate([ph, plo, ph], 1), jnp.concatenate([gh, gh, gl], 0), 1, 0
            )
            dq_ref[dev, h, q_rows, :] += dot(
                jnp.concatenate([dh, dl], 0), jnp.concatenate([k, k], 0), 0, 0
            )
        return carry

    lax.fori_loop(0, count, step, 0)


def local(
    queries,
    key_rows,
    value_rows,
    memory_keys,
    memory_values,
    gate_bias,
    norm_gain,
    block_ids,
    drop_seed,
    out_grad,
):
    heads_dev, shard_rows, head_width = queries.shape
    block_count = shard_rows // TB
    score_scale = 1.0 / math.sqrt(head_width)
    blk_count = lax.axis_size("blk")
    blk_index = lax.axis_index("blk")
    mem_rows = memory_keys.shape[1]
    mb_dev = mem_rows // TB
    gate_mix = jax.nn.sigmoid(gate_bias)[:, None, None]
    hb = 2 if heads_dev % 2 == 0 else 1
    prev_keys, prev_values = from_behind((key_rows, value_rows), "blk", 1)
    flat_ids = block_ids.reshape(1, -1)
    flat_ids = jnp.pad(flat_ids, ((0, 0), (0, -flat_ids.shape[1] % 128)))
    all_queries, ids_all = gather_blocks(queries, 1, flat_ids)

    smem = pl.BlockSpec(memory_space=pltpu.SMEM)
    grid = (heads_dev // hb,)
    q_spec = pl.BlockSpec((blk_count, hb, shard_rows, head_width), lambda i: (0, i, 0, 0))
    x_spec = pl.BlockSpec((blk_count, hb, shard_rows + EXTRA, head_width), lambda i: (0, i, 0, 0))
    m_spec = pl.BlockSpec((hb, mem_rows, head_width), lambda i: (i, 0, 0))
    params = pltpu.CompilerParams(vmem_limit_bytes=56 * 1024 * 1024)
    scratch = [pltpu.SMEM((blk_count * block_count * R + 1,), jnp.int32)]
    tile_flops = 2 * TB * TB * head_width * heads_dev * block_count * R
    partial = pl.pallas_call(
        functools.partial(far_forward, hb, mb_dev, block_count, score_scale),
        grid=grid,
        in_specs=[smem, q_spec, m_spec, m_spec],
        out_specs=x_spec,
        out_shape=jax.ShapeDtypeStruct(
            (blk_count, heads_dev, shard_rows + EXTRA, head_width), f32
        ),
        scratch_shapes=scratch,
        compiler_params=params,
        cost_estimate=pl.CostEstimate(
            flops=8 * tile_flops, bytes_accessed=12 * 2**20, transcendentals=0
        ),
        name="far_forward",
    )(ids_all, all_queries, memory_keys, memory_values)

    near_keys = jnp.concatenate([prev_keys, key_rows], 1)
    near_values = jnp.concatenate([prev_values, value_rows], 1)
    row_pos = jnp.arange(shard_rows, dtype=jnp.int32)[:, None]
    col_pos = jnp.arange(2 * shard_rows, dtype=jnp.int32)[None, :]
    in_window = (
        (col_pos > row_pos)
        & (col_pos <= row_pos + shard_rows)
        & (blk_index * shard_rows - shard_rows + col_pos >= 0)
    )
    near_scores = jnp.einsum("hqd,hkd->hqk", queries, near_keys, precision=high) * score_scale
    near_exp = jnp.where(in_window[None], jnp.exp(near_scores), 0.0)
    near_total = jnp.sum(near_exp, -1, keepdims=True)
    near_weights = near_exp / near_total
    local_out = jnp.einsum("hqk,hkd->hqd", near_weights, near_values, precision=high)

    whole = scatter_blocks(partial, 2, "scatter_out")
    far_total = whole[:, shard_rows : shard_rows + block_count].reshape(heads_dev, shard_rows, 1)
    memory_out = whole[:, :shard_rows] / far_total

    mixed = gate_mix * local_out + (1.0 - gate_mix) * memory_out
    shape = queries.shape
    head_base = lax.axis_index("head") * heads_dev
    token_base = blk_index * shard_rows
    counter = (
        (head_base + lax.broadcasted_iota(jnp.int32, shape, 0)) * (shard_rows * blk_count)
        + token_base
        + lax.broadcasted_iota(jnp.int32, shape, 1)
    ) * head_width + lax.broadcasted_iota(jnp.int32, shape, 2)
    keep = mix_bits(counter, drop_seed[0]).astype(f32)
    scaled_grad = norm_gain[:, None, :] * keep * out_grad
    sums = lax.psum(
        jnp.stack([jnp.sum(mixed * mixed, axis=(0, 2)), jnp.sum(scaled_grad * mixed, axis=(0, 2))]),
        "head",
    )
    feature_count = H * head_width
    inverse = lax.rsqrt(sums[0] / feature_count + norm_eps)[None, :, None]
    mixed_grad = (
        inverse * scaled_grad
        - mixed * inverse * inverse * inverse * (sums[1] / feature_count)[None, :, None]
    )
    near_grad = gate_mix * mixed_grad
    far_grad = (1.0 - gate_mix) * mixed_grad
    far_delta = jnp.sum(far_grad * memory_out, -1)
    tail = jnp.concatenate(
        [
            far_delta.reshape(heads_dev, block_count, TB),
            (1.0 / far_total).reshape(heads_dev, block_count, TB),
            jnp.zeros((heads_dev, EXTRA - 2 * block_count, TB), f32),
        ],
        1,
    )
    all_grad = gather_blocks(jnp.concatenate([far_grad, tail], 1), 3)
    dq_all, memory_key_grad, memory_value_grad = pl.pallas_call(
        functools.partial(far_backward, hb, mb_dev, block_count, score_scale),
        grid=grid,
        in_specs=[smem, q_spec, x_spec, m_spec, m_spec],
        out_specs=[q_spec, m_spec, m_spec],
        out_shape=[
            jax.ShapeDtypeStruct((blk_count, heads_dev, shard_rows, head_width), f32),
            jax.ShapeDtypeStruct((heads_dev, mem_rows, head_width), f32),
            jax.ShapeDtypeStruct((heads_dev, mem_rows, head_width), f32),
        ],
        scratch_shapes=scratch,
        compiler_params=params,
        cost_estimate=pl.CostEstimate(
            flops=24 * tile_flops, bytes_accessed=24 * 2**20, transcendentals=0
        ),
        name="far_backward",
    )(ids_all, all_queries, all_grad, memory_keys, memory_values)
    far_query_grad = scatter_blocks(dq_all, 4, "scatter_query_grad") * score_scale

    near_delta = jnp.sum(near_grad * local_out, -1, keepdims=True)
    near_dp = jnp.einsum("hqd,hkd->hqk", near_grad, near_values, precision=high)
    near_ds = near_weights * (near_dp - near_delta) * score_scale
    key_part = jnp.einsum("hqk,hqd->hkd", near_ds, queries, precision=high)
    value_part = jnp.einsum("hqk,hqd->hkd", near_weights, near_grad, precision=high)
    back_keys, back_values = from_behind(
        (key_part[:, :shard_rows], value_part[:, :shard_rows]), "blk", -1
    )
    key_grad = key_part[:, shard_rows:] + back_keys
    value_grad = value_part[:, shard_rows:] + back_values
    near_query_grad = jnp.einsum("hqk,hkd->hqd", near_ds, near_keys, precision=high)
    query_grad = near_query_grad + far_query_grad
    return (query_grad, key_grad, value_grad, memory_key_grad, memory_value_grad)


def solution(mesh):
    return jax.shard_map(
        local,
        mesh=mesh,
        in_specs=(
            P("head", "blk", None),
            P("head", "blk", None),
            P("head", "blk", None),
            P("head", "blk", None),
            P("head", "blk", None),
            P("head"),
            P("head", None),
            P("blk", None),
            P(),
            P("head", "blk", None),
        ),
        out_specs=(
            P("head", "blk", None),
            P("head", "blk", None),
            P("head", "blk", None),
            P("head", "blk", None),
            P("head", "blk", None),
        ),
        check_vma=False,
    )
```

```python
import functools
import math

import jax
import jax.numpy as jnp
from jax import lax
from jax.experimental import pallas as pl
from jax.experimental.pallas import tpu as pltpu
from jax.sharding import PartitionSpec as P

H = 16
TB = 128
R = 16
EXTRA = 8

high = lax.Precision.HIGH
drop_level = 103
norm_eps = 1e-06
bf16 = jnp.bfloat16
f32 = jnp.float32


def from_behind(x, axis, by):
    devices = lax.axis_size(axis)
    pairs = [(i, i + by) for i in range(devices) if 0 <= i + by < devices]
    return lax.ppermute(x, axis, pairs)


def mix_bits(counter, seed_value):
    state = counter * jnp.int32(-1640531535) + seed_value
    state = state ^ lax.shift_right_logical(state, jnp.int32(15))
    state = state * jnp.int32(739982445)
    state = state ^ lax.shift_right_logical(state, jnp.int32(12))
    state = state * jnp.int32(695872825)
    state = state ^ lax.shift_right_logical(state, jnp.int32(15))
    return jnp.where(state & 1023 >= drop_level, 1.0 / 0.9, 0.0)


def split(x):
    top = x.astype(bf16)
    return top, (x - top.astype(f32)).astype(bf16)


def dot(a, b, ca, cb):
    return lax.dot_general(a, b, (((ca,), (cb,)), ((), ())), preferred_element_type=f32)


def flip(index, bit):
    return index + bit - 2 * bit * ((index // bit) % 2)


def greet(others):
    barrier = pltpu.get_barrier_semaphore()
    for other in others:
        pl.semaphore_signal(
            barrier, inc=1, device_id={"blk": other}, device_id_type=pl.DeviceIdType.MESH
        )
    pl.semaphore_wait(barrier, len(others))


def sender(send_sems, recv_sems):
    def send(src, dst, index, other):
        copy = pltpu.make_async_remote_copy(
            src_ref=src,
            dst_ref=dst,
            send_sem=send_sems.at[index],
            recv_sem=recv_sems.at[index],
            device_id={"blk": other},
            device_id_type=pl.DeviceIdType.MESH,
        )
        copy.start()
        return copy

    return send


def gather_steps(x_ref, out_ref, send_sems, recv_sems, own_sem):
    me = lax.axis_index("blk")
    side, over_x, over_y = flip(me, 1), flip(me, 2), flip(me, 4)
    far = flip(over_x, 4)
    half = x_ref.shape[0] // 2
    low, high_part = pl.ds(0, half), pl.ds(half, half)
    send = sender(send_sems, recv_sems)
    to_x = send(x_ref, out_ref.at[me], 1, over_x)
    to_y = send(x_ref, out_ref.at[me], 2, over_y)
    to_side = send(x_ref, out_ref.at[me], 0, side)
    own = pltpu.make_async_copy(x_ref, out_ref.at[me], own_sem)
    own.start()
    to_x.wait_recv()
    x_to_y = send(out_ref.at[over_x, high_part], out_ref.at[over_x, high_part], 4, over_y)
    x_to_side = send(out_ref.at[over_x], out_ref.at[over_x], 3, side)
    to_y.wait_recv()
    y_to_x = send(out_ref.at[over_y, low], out_ref.at[over_y, low], 6, over_x)
    y_to_side = send(out_ref.at[over_y], out_ref.at[over_y], 5, side)
    y_to_x.wait_recv()
    low_to_side = send(out_ref.at[far, low], out_ref.at[far, low], 7, side)
    x_to_y.wait_recv()
    high_to_side = send(out_ref.at[far, high_part], out_ref.at[far, high_part], 8, side)
    for copy in (to_side, x_to_side, y_to_side, low_to_side, high_to_side):
        copy.wait()
    for copy in (to_x, to_y, x_to_y, y_to_x):
        copy.wait_send()
    own.wait()


def gather_ids_kernel(x_ref, ids_ref, out_ref, ids_out_ref, send_sems, recv_sems, id_send, id_recv, own_sems):
    me = lax.axis_index("blk")
    count = out_ref.shape[0]
    others = [(me + j) % count for j in range(1, count)]
    greet(others)
    own = pltpu.make_async_copy(ids_ref, ids_out_ref.at[me], own_sems.at[1])
    own.start()
    send = sender(id_send, id_recv)
    copies = [send(ids_ref, ids_out_ref.at[me], j, other) for j, other in enumerate(others)]
    gather_steps(x_ref, out_ref, send_sems, recv_sems, own_sems.at[0])
    for copy in copies:
        copy.wait()
    own.wait()


def gather_kernel(x_ref, out_ref, send_sems, recv_sems, own_sem):
    me = lax.axis_index("blk")
    greet([flip(me, 1), flip(me, 2), flip(me, 4)])
    gather_steps(x_ref, out_ref, send_sems, recv_sems, own_sem)


def gather_blocks(x, collective_id, ids=None):
    count = lax.axis_size("blk")
    if count != 8 or x.shape[0] % 2:
        gathered = lax.all_gather(x, "blk", axis=0)
        return gathered if ids is None else (gathered, lax.all_gather(ids, "blk", axis=0))
    whole = jax.ShapeDtypeStruct((count,) + x.shape, x.dtype)
    any_space = pl.BlockSpec(memory_space=pl.ANY)
    params = pltpu.CompilerParams(collective_id=collective_id, has_side_effects=True)
    sems = [pltpu.SemaphoreType.DMA((9,)), pltpu.SemaphoreType.DMA((9,))]
    cost = pl.CostEstimate(flops=0, bytes_accessed=2**26, transcendentals=0)
    if ids is None:
        return pl.pallas_call(
            gather_kernel,
            in_specs=[any_space],
            out_specs=any_space,
            out_shape=whole,
            scratch_shapes=sems + [pltpu.SemaphoreType.DMA],
            compiler_params=params,
            cost_estimate=cost,
            name="gather_grad",
        )(x)
    return pl.pallas_call(
        gather_ids_kernel,
        in_specs=[any_space, pl.BlockSpec(memory_space=pltpu.VMEM)],
        out_specs=[any_space, pl.BlockSpec(memory_space=pltpu.VMEM)],
        out_shape=[whole, jax.ShapeDtypeStruct((count,) + ids.shape, ids.dtype)],
        scratch_shapes=sems
        + [
            pltpu.SemaphoreType.DMA((count - 1,)),
            pltpu.SemaphoreType.DMA((count - 1,)),
            pltpu.SemaphoreType.DMA((2,)),
        ],
        compiler_params=params,
        cost_estimate=cost,
        name="gather_queries",
    )(x, ids)


def scatter_kernel(
    part_ref, out_ref, side_ref, far_ref, x_ref, y_ref, hop_ref, in_x_ref, in_y_ref, send_sems, recv_sems
):
    me = lax.axis_index("blk")
    side, over_x, over_y = flip(me, 1), flip(me, 2), flip(me, 4)
    far = flip(over_x, 4)
    half = out_ref.shape[0] // 2
    low, high_part = pl.ds(0, half), pl.ds(half, half)
    greet([side, over_x, over_y])
    send = sender(send_sems, recv_sems)
    far_in = send(part_ref.at[flip(far, 1)], side_ref.at[0], 0, side)
    x_in = send(part_ref.at[flip(over_x, 1)], side_ref.at[1], 1, side)
    y_in = send(part_ref.at[flip(over_y, 1)], side_ref.at[2], 2, side)
    own_in = send(part_ref.at[side], side_ref.at[3], 3, side)
    far_in.wait_recv()
    far_ref[...] = part_ref[far] + side_ref[0]
    far_to_x = send(far_ref.at[low], hop_ref.at[0], 4, over_x)
    far_to_y = send(far_ref.at[high_part], hop_ref.at[1], 5, over_y)
    x_in.wait_recv()
    x_ref[...] = part_ref[over_x] + side_ref[1]
    x_low = send(x_ref.at[low], in_x_ref.at[low], 6, over_x)
    y_in.wait_recv()
    y_ref[...] = part_ref[over_y] + side_ref[2]
    y_high = send(y_ref.at[high_part], in_y_ref.at[high_part], 7, over_y)
    far_to_y.wait_recv()
    x_ref[high_part] += hop_ref[1]
    x_high = send(x_ref.at[high_part], in_x_ref.at[high_part], 8, over_x)
    far_to_x.wait_recv()
    y_ref[low] += hop_ref[0]
    y_low = send(y_ref.at[low], in_y_ref.at[low], 9, over_y)
    own_in.wait_recv()
    out_ref[...] = part_ref[me] + side_ref[3]
    x_low.wait_recv()
    out_ref[low] += in_x_ref[low]
    y_high.wait_recv()
    out_ref[high_part] += in_y_ref[high_part]
    x_high.wait_recv()
    out_ref[high_part] += in_x_ref[high_part]
    y_low.wait_recv()
    out_ref[low] += in_y_ref[low]
    for copy in (far_in, x_in, y_in, own_in, far_to_x, far_to_y, x_low, y_high, x_high, y_low):
        copy.wait_send()


def scatter_blocks(parts, collective_id, name):
    count = lax.axis_size("blk")
    if count != 8 or parts.shape[1] % 2:
        return lax.psum_scatter(parts, "blk", scatter_dimension=0, tiled=False)
    shape = parts.shape[1:]
    block = pltpu.VMEM(shape, parts.dtype)
    return pl.pallas_call(
        scatter_kernel,
        in_specs=[pl.BlockSpec(memory_space=pltpu.VMEM)],
        out_specs=pl.BlockSpec(memory_space=pltpu.VMEM),
        out_shape=jax.ShapeDtypeStruct(shape, parts.dtype),
        scratch_shapes=[
            pltpu.VMEM((4,) + shape, parts.dtype),
            block,
            block,
            block,
            pltpu.VMEM((2, shape[0] // 2) + shape[1:], parts.dtype),
            block,
            block,
            pltpu.SemaphoreType.DMA((10,)),
            pltpu.SemaphoreType.DMA((10,)),
        ],
        compiler_params=pltpu.CompilerParams(
            collective_id=collective_id, has_side_effects=True, vmem_limit_bytes=40 * 1024 * 1024
        ),
        cost_estimate=pl.CostEstimate(flops=0, bytes_accessed=2**26, transcendentals=0),
        name=name,
    )(parts)


def collect_pairs(ids_ref, list_ref, mb_dev):
    me = lax.axis_index("blk")
    low = me * mb_dev
    total = ids_ref.shape[0]

    @pl.when(pl.program_id(0) == 0)
    def _():
        def scan(i, count):
            for j in range(8):
                at = i * 8 + j
                list_ref[count] = at
                ident = ids_ref[at]
                mine = (ident >= low) & (ident < low + mb_dev)
                count = count + mine.astype(jnp.int32)
            return count

        count = lax.fori_loop(0, total // 8, scan, jnp.int32(0))
        list_ref[total + 1] = count

    return list_ref[total + 1], low


def place(ids_ref, list_ref, low, block_count, i):
    at = list_ref[i]
    block = lax.div(at, jnp.int32(R))
    dev = lax.div(block, jnp.int32(block_count))
    sub = block - dev * block_count
    return dev, sub * TB, (ids_ref[at] - low) * TB, sub


def far_forward(heads, mb_dev, block_count, scale, ids_ref, q_ref, k_ref, v_ref, out_ref, list_ref):
    out_ref[...] = jnp.zeros_like(out_ref)
    count, low = collect_pairs(ids_ref, list_ref, mb_dev)
    rows = q_ref.shape[2]
    ones = jnp.ones((8, 2 * TB), bf16)

    def step(i, carry):
        dev, q_at, k_at, sub = place(ids_ref, list_ref, low, block_count, i)
        q_rows = pl.ds(pl.multiple_of(q_at, TB), TB)
        k_rows = pl.ds(pl.multiple_of(k_at, TB), TB)
        for h in range(heads):
            q2 = jnp.concatenate(split(q_ref[dev, h, q_rows, :] * scale), 1)
            k = k_ref[h, k_rows, :]
            v = v_ref[h, k_rows, :]
            e = jnp.exp(dot(q2, jnp.concatenate([k, k], 1), 1, 1))
            e2 = jnp.concatenate(split(e), 1)
            out_ref[dev, h, q_rows, :] += dot(e2, jnp.concatenate([v, v], 0), 1, 0)
            out_ref[dev, h, pl.ds(rows + sub, 1), :] += dot(ones, e2, 1, 1)[:1]
        return carry

    lax.fori_loop(0, count, step, 0)


def far_backward(
    heads, mb_dev, block_count, scale, ids_ref, q_ref, g_ref, k_ref, v_ref, dq_ref, dk_ref, dv_ref, list_ref
):
    dq_ref[...] = jnp.zeros_like(dq_ref)
    dk_ref[...] = jnp.zeros_like(dk_ref)
    dv_ref[...] = jnp.zeros_like(dv_ref)
    count, low = collect_pairs(ids_ref, list_ref, mb_dev)
    rows = q_ref.shape[2]

    def step(i, carry):
        dev, q_at, k_at, sub = place(ids_ref, list_ref, low, block_count, i)
        q_rows = pl.ds(pl.multiple_of(q_at, TB), TB)
        k_rows = pl.ds(pl.multiple_of(k_at, TB), TB)
        for h in range(heads):
            qh, ql = split(q_ref[dev, h, q_rows, :] * scale)
            gh, gl = split(g_ref[dev, h, q_rows, :])
            delta = g_ref[dev, h, pl.ds(rows + sub, 1), :]
            rden = g_ref[dev, h, pl.ds(rows + block_count + sub, 1), :]
            k = k_ref[h, k_rows, :]
            v = v_ref[h, k_rows, :]
            st = dot(jnp.concatenate([k, k], 1), jnp.concatenate([qh, ql], 1), 1, 1)
            dp = dot(jnp.concatenate([v, v], 1), jnp.concatenate([gh, gl], 1), 1, 1)
            p = jnp.exp(st) * rden
            ds = p * (dp - delta)
            ph, plo = split(p)
            dh, dl = split(ds)
            dk_ref[h, k_rows, :] += dot(
                jnp.concatenate([dh, dl, dh], 1), jnp.concatenate([qh, qh, ql], 0), 1, 0
            )
            dv_ref[h, k_rows, :] += dot(
                jnp.concatenate([ph, plo, ph], 1), jnp.concatenate([gh, gh, gl], 0), 1, 0
            )
            dq_ref[dev, h, q_rows, :] += dot(
                jnp.concatenate([dh, dl], 0), jnp.concatenate([k, k], 0), 0, 0
            )
        return carry

    lax.fori_loop(0, count, step, 0)


def local(
    queries,
    key_rows,
    value_rows,
    memory_keys,
    memory_values,
    gate_bias,
    norm_gain,
    block_ids,
    drop_seed,
    out_grad,
):
    heads_dev, shard_rows, head_width = queries.shape
    block_count = shard_rows // TB
    score_scale = 1.0 / math.sqrt(head_width)
    blk_count = lax.axis_size("blk")
    blk_index = lax.axis_index("blk")
    mem_rows = memory_keys.shape[1]
    mb_dev = mem_rows // TB
    gate_mix = jax.nn.sigmoid(gate_bias)[:, None, None]
    hb = 2 if heads_dev % 2 == 0 else 1
    prev_keys, prev_values = from_behind((key_rows, value_rows), "blk", 1)
    flat_ids = block_ids.reshape(1, -1)
    flat_ids = jnp.pad(flat_ids, ((0, 0), (0, -flat_ids.shape[1] % 128)))
    all_queries, ids_all = gather_blocks(queries, 1, flat_ids)
    ids_all = ids_all[:, 0, : block_count * R].reshape(-1)

    smem = pl.BlockSpec(memory_space=pltpu.SMEM)
    grid = (heads_dev // hb,)
    q_spec = pl.BlockSpec((blk_count, hb, shard_rows, head_width), lambda i: (0, i, 0, 0))
    x_spec = pl.BlockSpec((blk_count, hb, shard_rows + EXTRA, head_width), lambda i: (0, i, 0, 0))
    m_spec = pl.BlockSpec((hb, mem_rows, head_width), lambda i: (i, 0, 0))
    params = pltpu.CompilerParams(vmem_limit_bytes=56 * 1024 * 1024)
    scratch = [pltpu.SMEM((blk_count * block_count * R + 2,), jnp.int32)]
    tile_flops = 2 * TB * TB * head_width * heads_dev * block_count * R
    partial = pl.pallas_call(
        functools.partial(far_forward, hb, mb_dev, block_count, score_scale),
        grid=grid,
        in_specs=[smem, q_spec, m_spec, m_spec],
        out_specs=x_spec,
        out_shape=jax.ShapeDtypeStruct(
            (blk_count, heads_dev, shard_rows + EXTRA, head_width), f32
        ),
        scratch_shapes=scratch,
        compiler_params=params,
        cost_estimate=pl.CostEstimate(
            flops=8 * tile_flops, bytes_accessed=12 * 2**20, transcendentals=0
        ),
        name="far_forward",
    )(ids_all, all_queries, memory_keys, memory_values)

    near_keys = jnp.concatenate([prev_keys, key_rows], 1)
    near_values = jnp.concatenate([prev_values, value_rows], 1)
    row_pos = jnp.arange(shard_rows, dtype=jnp.int32)[:, None]
    col_pos = jnp.arange(2 * shard_rows, dtype=jnp.int32)[None, :]
    in_window = (
        (col_pos > row_pos)
        & (col_pos <= row_pos + shard_rows)
        & (blk_index * shard_rows - shard_rows + col_pos >= 0)
    )
    near_scores = jnp.einsum("hqd,hkd->hqk", queries, near_keys, precision=high) * score_scale
    near_exp = jnp.where(in_window[None], jnp.exp(near_scores), 0.0)
    near_total = jnp.sum(near_exp, -1, keepdims=True)
    near_weights = near_exp / near_total
    local_out = jnp.einsum("hqk,hkd->hqd", near_weights, near_values, precision=high)

    whole = scatter_blocks(partial, 2, "scatter_out")
    far_total = whole[:, shard_rows : shard_rows + block_count].reshape(heads_dev, shard_rows, 1)
    memory_out = whole[:, :shard_rows] / far_total

    mixed = gate_mix * local_out + (1.0 - gate_mix) * memory_out
    shape = queries.shape
    head_base = lax.axis_index("head") * heads_dev
    token_base = blk_index * shard_rows
    counter = (
        (head_base + lax.broadcasted_iota(jnp.int32, shape, 0)) * (shard_rows * blk_count)
        + token_base
        + lax.broadcasted_iota(jnp.int32, shape, 1)
    ) * head_width + lax.broadcasted_iota(jnp.int32, shape, 2)
    keep = mix_bits(counter, drop_seed[0]).astype(f32)
    scaled_grad = norm_gain[:, None, :] * keep * out_grad
    sums = lax.psum(
        jnp.stack([jnp.sum(mixed * mixed, axis=(0, 2)), jnp.sum(scaled_grad * mixed, axis=(0, 2))]),
        "head",
    )
    feature_count = H * head_width
    inverse = lax.rsqrt(sums[0] / feature_count + norm_eps)[None, :, None]
    mixed_grad = (
        inverse * scaled_grad
        - mixed * inverse * inverse * inverse * (sums[1] / feature_count)[None, :, None]
    )
    near_grad = gate_mix * mixed_grad
    far_grad = (1.0 - gate_mix) * mixed_grad
    far_delta = jnp.sum(far_grad * memory_out, -1)
    tail = jnp.concatenate(
        [
            far_delta.reshape(heads_dev, block_count, TB),
            (1.0 / far_total).reshape(heads_dev, block_count, TB),
            jnp.zeros((heads_dev, EXTRA - 2 * block_count, TB), f32),
        ],
        1,
    )
    all_grad = gather_blocks(jnp.concatenate([far_grad, tail], 1), 3)
    dq_all, memory_key_grad, memory_value_grad = pl.pallas_call(
        functools.partial(far_backward, hb, mb_dev, block_count, score_scale),
        grid=grid,
        in_specs=[smem, q_spec, x_spec, m_spec, m_spec],
        out_specs=[q_spec, m_spec, m_spec],
        out_shape=[
            jax.ShapeDtypeStruct((blk_count, heads_dev, shard_rows, head_width), f32),
            jax.ShapeDtypeStruct((heads_dev, mem_rows, head_width), f32),
            jax.ShapeDtypeStruct((heads_dev, mem_rows, head_width), f32),
        ],
        scratch_shapes=scratch,
        compiler_params=params,
        cost_estimate=pl.CostEstimate(
            flops=24 * tile_flops, bytes_accessed=24 * 2**20, transcendentals=0
        ),
        name="far_backward",
    )(ids_all, all_queries, all_grad, memory_keys, memory_values)
    far_query_grad = scatter_blocks(dq_all, 4, "scatter_query_grad") * score_scale

    near_delta = jnp.sum(near_grad * local_out, -1, keepdims=True)
    near_dp = jnp.einsum("hqd,hkd->hqk", near_grad, near_values, precision=high)
    near_ds = near_weights * (near_dp - near_delta) * score_scale
    key_part = jnp.einsum("hqk,hqd->hkd", near_ds, queries, precision=high)
    value_part = jnp.einsum("hqk,hqd->hkd", near_weights, near_grad, precision=high)
    back_keys, back_values = from_behind(
        (key_part[:, :shard_rows], value_part[:, :shard_rows]), "blk", -1
    )
    key_grad = key_part[:, shard_rows:] + back_keys
    value_grad = value_part[:, shard_rows:] + back_values
    near_query_grad = jnp.einsum("hqk,hkd->hqd", near_ds, near_keys, precision=high)
    query_grad = near_query_grad + far_query_grad
    return (query_grad, key_grad, value_grad, memory_key_grad, memory_value_grad)


def solution(mesh):
    return jax.shard_map(
        local,
        mesh=mesh,
        in_specs=(
            P("head", "blk", None),
            P("head", "blk", None),
            P("head", "blk", None),
            P("head", "blk", None),
            P("head", "blk", None),
            P("head"),
            P("head", None),
            P("blk", None),
            P(),
            P("head", "blk", None),
        ),
        out_specs=(
            P("head", "blk", None),
            P("head", "blk", None),
            P("head", "blk", None),
            P("head", "blk", None),
            P("head", "blk", None),
        ),
        check_vma=False,
    )
```

```python
import functools
import math

import jax
import jax.numpy as jnp
from jax import lax
from jax.experimental import pallas as pl
from jax.experimental.pallas import tpu as pltpu
from jax.sharding import PartitionSpec as P

H = 16
TB = 128
R = 16
EXTRA = 8

high = lax.Precision.HIGH
drop_level = 103
norm_eps = 1e-06
bf16 = jnp.bfloat16
f32 = jnp.float32


def from_behind(x, axis, by):
    devices = lax.axis_size(axis)
    pairs = [(i, i + by) for i in range(devices) if 0 <= i + by < devices]
    return lax.ppermute(x, axis, pairs)


def mix_bits(counter, seed_value):
    state = counter * jnp.int32(-1640531535) + seed_value
    state = state ^ lax.shift_right_logical(state, jnp.int32(15))
    state = state * jnp.int32(739982445)
    state = state ^ lax.shift_right_logical(state, jnp.int32(12))
    state = state * jnp.int32(695872825)
    state = state ^ lax.shift_right_logical(state, jnp.int32(15))
    return jnp.where(state & 1023 >= drop_level, 1.0 / 0.9, 0.0)


def split(x):
    top = x.astype(bf16)
    return top, (x - top.astype(f32)).astype(bf16)


def dot(a, b, ca, cb):
    return lax.dot_general(a, b, (((ca,), (cb,)), ((), ())), preferred_element_type=f32)


def flip(index, bit):
    return index + bit - 2 * bit * ((index // bit) % 2)


def greet(others):
    barrier = pltpu.get_barrier_semaphore()
    for other in others:
        pl.semaphore_signal(
            barrier, inc=1, device_id={"blk": other}, device_id_type=pl.DeviceIdType.MESH
        )
    pl.semaphore_wait(barrier, len(others))


def sender(send_sems, recv_sems):
    def send(src, dst, index, other):
        copy = pltpu.make_async_remote_copy(
            src_ref=src,
            dst_ref=dst,
            send_sem=send_sems.at[index],
            recv_sem=recv_sems.at[index],
            device_id={"blk": other},
            device_id_type=pl.DeviceIdType.MESH,
        )
        copy.start()
        return copy

    return send


def gather_steps(x_ref, out_ref, send_sems, recv_sems, own_sem):
    me = lax.axis_index("blk")
    side, over_x, over_y = flip(me, 1), flip(me, 2), flip(me, 4)
    far = flip(over_x, 4)
    half = x_ref.shape[0] // 2
    low, high_part = pl.ds(0, half), pl.ds(half, half)
    send = sender(send_sems, recv_sems)
    to_x = send(x_ref, out_ref.at[me], 1, over_x)
    to_y = send(x_ref, out_ref.at[me], 2, over_y)
    to_side = send(x_ref, out_ref.at[me], 0, side)
    own = pltpu.make_async_copy(x_ref, out_ref.at[me], own_sem)
    own.start()
    to_x.wait_recv()
    x_to_y = send(out_ref.at[over_x, high_part], out_ref.at[over_x, high_part], 4, over_y)
    x_to_side = send(out_ref.at[over_x], out_ref.at[over_x], 3, side)
    to_y.wait_recv()
    y_to_x = send(out_ref.at[over_y, low], out_ref.at[over_y, low], 6, over_x)
    y_to_side = send(out_ref.at[over_y], out_ref.at[over_y], 5, side)
    y_to_x.wait_recv()
    low_to_side = send(out_ref.at[far, low], out_ref.at[far, low], 7, side)
    x_to_y.wait_recv()
    high_to_side = send(out_ref.at[far, high_part], out_ref.at[far, high_part], 8, side)
    for copy in (to_side, x_to_side, y_to_side, low_to_side, high_to_side):
        copy.wait()
    for copy in (to_x, to_y, x_to_y, y_to_x):
        copy.wait_send()
    own.wait()


def gather_ids_kernel(x_ref, ids_ref, out_ref, ids_out_ref, send_sems, recv_sems, id_send, id_recv, own_sems):
    me = lax.axis_index("blk")
    count = out_ref.shape[0]
    others = [(me + j) % count for j in range(1, count)]
    greet(others)
    own = pltpu.make_async_copy(ids_ref, ids_out_ref.at[me], own_sems.at[1])
    own.start()
    send = sender(id_send, id_recv)
    copies = [send(ids_ref, ids_out_ref.at[me], j, other) for j, other in enumerate(others)]
    gather_steps(x_ref, out_ref, send_sems, recv_sems, own_sems.at[0])
    for copy in copies:
        copy.wait()
    own.wait()


def gather_kernel(x_ref, out_ref, send_sems, recv_sems, own_sem):
    me = lax.axis_index("blk")
    greet([flip(me, 1), flip(me, 2), flip(me, 4)])
    gather_steps(x_ref, out_ref, send_sems, recv_sems, own_sem)


def gather_blocks(x, collective_id, ids=None):
    count = lax.axis_size("blk")
    if count != 8 or x.shape[0] % 2:
        gathered = lax.all_gather(x, "blk", axis=0)
        return gathered if ids is None else (gathered, lax.all_gather(ids, "blk", axis=0))
    whole = jax.ShapeDtypeStruct((count,) + x.shape, x.dtype)
    any_space = pl.BlockSpec(memory_space=pl.ANY)
    params = pltpu.CompilerParams(collective_id=collective_id, has_side_effects=True)
    sems = [pltpu.SemaphoreType.DMA((9,)), pltpu.SemaphoreType.DMA((9,))]
    cost = pl.CostEstimate(flops=0, bytes_accessed=2**26, transcendentals=0)
    if ids is None:
        return pl.pallas_call(
            gather_kernel,
            in_specs=[any_space],
            out_specs=any_space,
            out_shape=whole,
            scratch_shapes=sems + [pltpu.SemaphoreType.DMA],
            compiler_params=params,
            cost_estimate=cost,
            name="gather_grad",
        )(x)
    return pl.pallas_call(
        gather_ids_kernel,
        in_specs=[any_space, pl.BlockSpec(memory_space=pltpu.VMEM)],
        out_specs=[any_space, pl.BlockSpec(memory_space=pltpu.VMEM)],
        out_shape=[whole, jax.ShapeDtypeStruct((count,) + ids.shape, ids.dtype)],
        scratch_shapes=sems
        + [
            pltpu.SemaphoreType.DMA((count - 1,)),
            pltpu.SemaphoreType.DMA((count - 1,)),
            pltpu.SemaphoreType.DMA((2,)),
        ],
        compiler_params=params,
        cost_estimate=cost,
        name="gather_queries",
    )(x, ids)


def scatter_kernel(
    part_ref, out_ref, side_ref, far_ref, x_ref, y_ref, hop_ref, in_x_ref, in_y_ref, send_sems, recv_sems
):
    me = lax.axis_index("blk")
    side, over_x, over_y = flip(me, 1), flip(me, 2), flip(me, 4)
    far = flip(over_x, 4)
    half = out_ref.shape[0] // 2
    low, high_part = pl.ds(0, half), pl.ds(half, half)
    greet([side, over_x, over_y])
    send = sender(send_sems, recv_sems)
    far_in = send(part_ref.at[flip(far, 1)], side_ref.at[0], 0, side)
    x_in = send(part_ref.at[flip(over_x, 1)], side_ref.at[1], 1, side)
    y_in = send(part_ref.at[flip(over_y, 1)], side_ref.at[2], 2, side)
    own_in = send(part_ref.at[side], side_ref.at[3], 3, side)
    far_in.wait_recv()
    far_ref[...] = part_ref[far] + side_ref[0]
    far_to_x = send(far_ref.at[low], hop_ref.at[0], 4, over_x)
    far_to_y = send(far_ref.at[high_part], hop_ref.at[1], 5, over_y)
    x_in.wait_recv()
    x_ref[...] = part_ref[over_x] + side_ref[1]
    x_low = send(x_ref.at[low], in_x_ref.at[low], 6, over_x)
    y_in.wait_recv()
    y_ref[...] = part_ref[over_y] + side_ref[2]
    y_high = send(y_ref.at[high_part], in_y_ref.at[high_part], 7, over_y)
    far_to_y.wait_recv()
    x_ref[high_part] += hop_ref[1]
    x_high = send(x_ref.at[high_part], in_x_ref.at[high_part], 8, over_x)
    far_to_x.wait_recv()
    y_ref[low] += hop_ref[0]
    y_low = send(y_ref.at[low], in_y_ref.at[low], 9, over_y)
    own_in.wait_recv()
    out_ref[...] = part_ref[me] + side_ref[3]
    x_low.wait_recv()
    out_ref[low] += in_x_ref[low]
    y_high.wait_recv()
    out_ref[high_part] += in_y_ref[high_part]
    x_high.wait_recv()
    out_ref[high_part] += in_x_ref[high_part]
    y_low.wait_recv()
    out_ref[low] += in_y_ref[low]
    for copy in (far_in, x_in, y_in, own_in, far_to_x, far_to_y, x_low, y_high, x_high, y_low):
        copy.wait_send()


def scatter_blocks(parts, collective_id, name):
    count = lax.axis_size("blk")
    if count != 8 or parts.shape[1] % 2:
        return lax.psum_scatter(parts, "blk", scatter_dimension=0, tiled=False)
    shape = parts.shape[1:]
    block = pltpu.VMEM(shape, parts.dtype)
    return pl.pallas_call(
        scatter_kernel,
        in_specs=[pl.BlockSpec(memory_space=pltpu.VMEM)],
        out_specs=pl.BlockSpec(memory_space=pltpu.VMEM),
        out_shape=jax.ShapeDtypeStruct(shape, parts.dtype),
        scratch_shapes=[
            pltpu.VMEM((4,) + shape, parts.dtype),
            block,
            block,
            block,
            pltpu.VMEM((2, shape[0] // 2) + shape[1:], parts.dtype),
            block,
            block,
            pltpu.SemaphoreType.DMA((10,)),
            pltpu.SemaphoreType.DMA((10,)),
        ],
        compiler_params=pltpu.CompilerParams(
            collective_id=collective_id, has_side_effects=True, vmem_limit_bytes=40 * 1024 * 1024
        ),
        cost_estimate=pl.CostEstimate(flops=0, bytes_accessed=2**26, transcendentals=0),
        name=name,
    )(parts)


def collect_pairs(ids_ref, list_ref, mb_dev):
    me = lax.axis_index("blk")
    low = me * mb_dev
    total = ids_ref.shape[0]

    @pl.when(pl.program_id(0) == 0)
    def _():
        def scan(i, count):
            for j in range(8):
                at = i * 8 + j
                list_ref[count] = at
                ident = ids_ref[at]
                mine = (ident >= low) & (ident < low + mb_dev)
                count = count + mine.astype(jnp.int32)
            return count

        count = lax.fori_loop(0, total // 8, scan, jnp.int32(0))
        list_ref[total + 1] = count

    return list_ref[total + 1], low


def place(ids_ref, list_ref, low, block_count, i):
    at = list_ref[i]
    block = lax.div(at, jnp.int32(R))
    dev = lax.div(block, jnp.int32(block_count))
    sub = block - dev * block_count
    return dev, sub * TB, (ids_ref[at] - low) * TB, sub


def far_forward(heads, mb_dev, block_count, scale, ids_ref, q_ref, k_ref, v_ref, out_ref, list_ref):
    out_ref[...] = jnp.zeros_like(out_ref)
    count, low = collect_pairs(ids_ref, list_ref, mb_dev)
    rows = q_ref.shape[2]
    ones = jnp.ones((8, 2 * TB), bf16)

    def step(i, carry):
        dev, q_at, k_at, sub = place(ids_ref, list_ref, low, block_count, i)
        q_rows = pl.ds(pl.multiple_of(q_at, TB), TB)
        k_rows = pl.ds(pl.multiple_of(k_at, TB), TB)
        hs = range(heads)
        twice = [jnp.concatenate(split(q_ref[dev, h, q_rows, :] * scale), 1) for h in hs]
        ks = [k_ref[h, k_rows, :] for h in hs]
        vs = [v_ref[h, k_rows, :] for h in hs]
        scores = [dot(twice[h], jnp.concatenate([ks[h], ks[h]], 1), 1, 1) for h in hs]
        e2 = [jnp.concatenate(split(jnp.exp(scores[h])), 1) for h in hs]
        sums = [dot(e2[h], jnp.concatenate([vs[h], vs[h]], 0), 1, 0) for h in hs]
        totals = [dot(ones, e2[h], 1, 1)[:1] for h in hs]
        for h in hs:
            out_ref[dev, h, q_rows, :] += sums[h]
            out_ref[dev, h, pl.ds(rows + sub, 1), :] += totals[h]
        return carry

    lax.fori_loop(0, count, step, 0)


def far_backward(
    heads, mb_dev, block_count, scale, ids_ref, q_ref, g_ref, k_ref, v_ref, dq_ref, dk_ref, dv_ref, list_ref
):
    dq_ref[...] = jnp.zeros_like(dq_ref)
    dk_ref[...] = jnp.zeros_like(dk_ref)
    dv_ref[...] = jnp.zeros_like(dv_ref)
    count, low = collect_pairs(ids_ref, list_ref, mb_dev)
    rows = q_ref.shape[2]

    def step(i, carry):
        dev, q_at, k_at, sub = place(ids_ref, list_ref, low, block_count, i)
        q_rows = pl.ds(pl.multiple_of(q_at, TB), TB)
        k_rows = pl.ds(pl.multiple_of(k_at, TB), TB)
        hs = range(heads)
        q = [split(q_ref[dev, h, q_rows, :] * scale) for h in hs]
        g = [split(g_ref[dev, h, q_rows, :]) for h in hs]
        delta = [g_ref[dev, h, pl.ds(rows + sub, 1), :] for h in hs]
        rden = [g_ref[dev, h, pl.ds(rows + block_count + sub, 1), :] for h in hs]
        ks = [k_ref[h, k_rows, :] for h in hs]
        vs = [v_ref[h, k_rows, :] for h in hs]
        st = [dot(jnp.concatenate([ks[h], ks[h]], 1), jnp.concatenate(q[h], 1), 1, 1) for h in hs]
        dp = [dot(jnp.concatenate([vs[h], vs[h]], 1), jnp.concatenate(g[h], 1), 1, 1) for h in hs]
        weights = [jnp.exp(st[h]) * rden[h] for h in hs]
        ds = [split(weights[h] * (dp[h] - delta[h])) for h in hs]
        ps = [split(weights[h]) for h in hs]

        def three(x, y):
            return dot(
                jnp.concatenate([x[0], x[1], x[0]], 1), jnp.concatenate([y[0], y[0], y[1]], 0), 1, 0
            )

        dv = [three(ps[h], g[h]) for h in hs]
        dk = [three(ds[h], q[h]) for h in hs]
        dq = [
            dot(jnp.concatenate(ds[h], 0), jnp.concatenate([ks[h], ks[h]], 0), 0, 0) for h in hs
        ]
        for h in hs:
            dv_ref[h, k_rows, :] += dv[h]
            dk_ref[h, k_rows, :] += dk[h]
            dq_ref[dev, h, q_rows, :] += dq[h]
        return carry

    lax.fori_loop(0, count, step, 0)


def local(
    queries,
    key_rows,
    value_rows,
    memory_keys,
    memory_values,
    gate_bias,
    norm_gain,
    block_ids,
    drop_seed,
    out_grad,
):
    heads_dev, shard_rows, head_width = queries.shape
    block_count = shard_rows // TB
    score_scale = 1.0 / math.sqrt(head_width)
    blk_count = lax.axis_size("blk")
    blk_index = lax.axis_index("blk")
    mem_rows = memory_keys.shape[1]
    mb_dev = mem_rows // TB
    gate_mix = jax.nn.sigmoid(gate_bias)[:, None, None]
    hb = 2 if heads_dev % 2 == 0 else 1
    prev_keys, prev_values = from_behind((key_rows, value_rows), "blk", 1)
    flat_ids = block_ids.reshape(1, -1)
    flat_ids = jnp.pad(flat_ids, ((0, 0), (0, -flat_ids.shape[1] % 128)))
    all_queries, ids_all = gather_blocks(queries, 1, flat_ids)
    ids_all = ids_all[:, 0, : block_count * R].reshape(-1)

    smem = pl.BlockSpec(memory_space=pltpu.SMEM)
    grid = (heads_dev // hb,)
    q_spec = pl.BlockSpec((blk_count, hb, shard_rows, head_width), lambda i: (0, i, 0, 0))
    x_spec = pl.BlockSpec((blk_count, hb, shard_rows + EXTRA, head_width), lambda i: (0, i, 0, 0))
    m_spec = pl.BlockSpec((hb, mem_rows, head_width), lambda i: (i, 0, 0))
    params = pltpu.CompilerParams(vmem_limit_bytes=56 * 1024 * 1024)
    scratch = [pltpu.SMEM((blk_count * block_count * R + 2,), jnp.int32)]
    tile_flops = 2 * TB * TB * head_width * heads_dev * block_count * R
    partial = pl.pallas_call(
        functools.partial(far_forward, hb, mb_dev, block_count, score_scale),
        grid=grid,
        in_specs=[smem, q_spec, m_spec, m_spec],
        out_specs=x_spec,
        out_shape=jax.ShapeDtypeStruct(
            (blk_count, heads_dev, shard_rows + EXTRA, head_width), f32
        ),
        scratch_shapes=scratch,
        compiler_params=params,
        cost_estimate=pl.CostEstimate(
            flops=8 * tile_flops, bytes_accessed=12 * 2**20, transcendentals=0
        ),
        name="far_forward",
    )(ids_all, all_queries, memory_keys, memory_values)

    near_keys = jnp.concatenate([prev_keys, key_rows], 1)
    near_values = jnp.concatenate([prev_values, value_rows], 1)
    row_pos = jnp.arange(shard_rows, dtype=jnp.int32)[:, None]
    col_pos = jnp.arange(2 * shard_rows, dtype=jnp.int32)[None, :]
    in_window = (
        (col_pos > row_pos)
        & (col_pos <= row_pos + shard_rows)
        & (blk_index * shard_rows - shard_rows + col_pos >= 0)
    )
    near_scores = jnp.einsum("hqd,hkd->hqk", queries, near_keys, precision=high) * score_scale
    near_exp = jnp.where(in_window[None], jnp.exp(near_scores), 0.0)
    near_total = jnp.sum(near_exp, -1, keepdims=True)
    near_weights = near_exp / near_total
    local_out = jnp.einsum("hqk,hkd->hqd", near_weights, near_values, precision=high)

    whole = scatter_blocks(partial, 2, "scatter_out")
    far_total = whole[:, shard_rows : shard_rows + block_count].reshape(heads_dev, shard_rows, 1)
    memory_out = whole[:, :shard_rows] / far_total

    mixed = gate_mix * local_out + (1.0 - gate_mix) * memory_out
    shape = queries.shape
    head_base = lax.axis_index("head") * heads_dev
    token_base = blk_index * shard_rows
    counter = (
        (head_base + lax.broadcasted_iota(jnp.int32, shape, 0)) * (shard_rows * blk_count)
        + token_base
        + lax.broadcasted_iota(jnp.int32, shape, 1)
    ) * head_width + lax.broadcasted_iota(jnp.int32, shape, 2)
    keep = mix_bits(counter, drop_seed[0]).astype(f32)
    scaled_grad = norm_gain[:, None, :] * keep * out_grad
    sums = lax.psum(
        jnp.stack([jnp.sum(mixed * mixed, axis=(0, 2)), jnp.sum(scaled_grad * mixed, axis=(0, 2))]),
        "head",
    )
    feature_count = H * head_width
    inverse = lax.rsqrt(sums[0] / feature_count + norm_eps)[None, :, None]
    mixed_grad = (
        inverse * scaled_grad
        - mixed * inverse * inverse * inverse * (sums[1] / feature_count)[None, :, None]
    )
    near_grad = gate_mix * mixed_grad
    far_grad = (1.0 - gate_mix) * mixed_grad
    far_delta = jnp.sum(far_grad * memory_out, -1)
    tail = jnp.concatenate(
        [
            far_delta.reshape(heads_dev, block_count, TB),
            (1.0 / far_total).reshape(heads_dev, block_count, TB),
            jnp.zeros((heads_dev, EXTRA - 2 * block_count, TB), f32),
        ],
        1,
    )
    all_grad = gather_blocks(jnp.concatenate([far_grad, tail], 1), 3)
    dq_all, memory_key_grad, memory_value_grad = pl.pallas_call(
        functools.partial(far_backward, hb, mb_dev, block_count, score_scale),
        grid=grid,
        in_specs=[smem, q_spec, x_spec, m_spec, m_spec],
        out_specs=[q_spec, m_spec, m_spec],
        out_shape=[
            jax.ShapeDtypeStruct((blk_count, heads_dev, shard_rows, head_width), f32),
            jax.ShapeDtypeStruct((heads_dev, mem_rows, head_width), f32),
            jax.ShapeDtypeStruct((heads_dev, mem_rows, head_width), f32),
        ],
        scratch_shapes=scratch,
        compiler_params=params,
        cost_estimate=pl.CostEstimate(
            flops=24 * tile_flops, bytes_accessed=24 * 2**20, transcendentals=0
        ),
        name="far_backward",
    )(ids_all, all_queries, all_grad, memory_keys, memory_values)
    far_query_grad = scatter_blocks(dq_all, 4, "scatter_query_grad") * score_scale

    near_delta = jnp.sum(near_grad * local_out, -1, keepdims=True)
    near_dp = jnp.einsum("hqd,hkd->hqk", near_grad, near_values, precision=high)
    near_ds = near_weights * (near_dp - near_delta) * score_scale
    key_part = jnp.einsum("hqk,hqd->hkd", near_ds, queries, precision=high)
    value_part = jnp.einsum("hqk,hqd->hkd", near_weights, near_grad, precision=high)
    back_keys, back_values = from_behind(
        (key_part[:, :shard_rows], value_part[:, :shard_rows]), "blk", -1
    )
    key_grad = key_part[:, shard_rows:] + back_keys
    value_grad = value_part[:, shard_rows:] + back_values
    near_query_grad = jnp.einsum("hqk,hkd->hqd", near_ds, near_keys, precision=high)
    query_grad = near_query_grad + far_query_grad
    return (query_grad, key_grad, value_grad, memory_key_grad, memory_value_grad)


def solution(mesh):
    return jax.shard_map(
        local,
        mesh=mesh,
        in_specs=(
            P("head", "blk", None),
            P("head", "blk", None),
            P("head", "blk", None),
            P("head", "blk", None),
            P("head", "blk", None),
            P("head"),
            P("head", None),
            P("blk", None),
            P(),
            P("head", "blk", None),
        ),
        out_specs=(
            P("head", "blk", None),
            P("head", "blk", None),
            P("head", "blk", None),
            P("head", "blk", None),
            P("head", "blk", None),
        ),
        check_vma=False,
    )
```
